32 devices in a mesh: seq: 8 (over z, core), tp: 4 (over y, x).
Axes of the slice: x: 2, y: 2, z: 4, core: 2. Of those that a mesh axis runs over, the one named last changes fastest.
Arguments:
- layer_input: bfloat16 [8, 512, 4096], P('seq')
- memory: bfloat16 [8, 512, 4096], P('seq'), may hold values from -6 to 6
- seg_lengths: int32 [8], replicated, may hold values from 257 to 512, as said below
- query_weight: bfloat16 [4096, 4096], P(None, 'tp')
- key_weight: bfloat16 [4096, 4096], P(None, 'tp')
- value_weight: bfloat16 [4096, 4096], P(None, 'tp'), may hold values from -0.09375 to 0.09375
- out_weight: bfloat16 [4096, 4096], P('tp'), may hold values from -0.1875 to 0.1875
Outputs:
- attended: bfloat16 [8, 512, 4096], P('seq', 'tp')
The draws below stay inside these ranges and needn't reach their ends.
Inputs may be any that keep to these rules, and one draw needn't show every extreme that they name: `seg_lengths`: slots below a segment's count hold real tokens.
All inputs are finite; a program needn't handle non-finite values.
Results may differ from the reference program's by a relative error of at most 0.011.
Values may be sent and summed in bfloat16 or wider, within the bound.
No kernel may reach another device: no remote copies, remote signals or barrier semaphores. Data moves between devices by JAX's collectives and lax.ppermute only.
A program may use at most 128 MiB of HBM per device.

```python
import math
import jax
import jax.numpy as jnp
from jax import lax

D = 4096
HEADS = 32
HEAD_DIM = 128
SEG = 512
SEGS_DEV = 1
NSEGS = 8
N_SEQ = 8


def attention_pair(key):
    base = jax.random.normal(jax.random.fold_in(key, 11), (D, D), jnp.float32)
    other = jax.random.normal(jax.random.fold_in(key, 12), (D, D), jnp.float32)
    return (base, other)


def draw_query_weight(key, part):
    base, other = attention_pair(key)
    return (base * (1.5 / math.sqrt(D))).astype(jnp.bfloat16)


def draw_key_weight(key, part):
    base, other = attention_pair(key)
    mixed = other
    return (mixed * (1.5 / math.sqrt(D))).astype(jnp.bfloat16)


def draw_layer_input(key, part):
    states = jax.random.truncated_normal(jax.random.fold_in(key, 21), -6.0, 6.0, (NSEGS, SEG, D), jnp.float32)
    return states.astype(jnp.bfloat16)


def draw_seg_lengths(key, part):
    short_by = jax.random.randint(jax.random.fold_in(key, 31), (NSEGS,), 0, SEG // 2)
    first_pick = jax.random.randint(jax.random.fold_in(key, 32), (), 0, NSEGS)
    second_pick = jnp.mod(first_pick + 1 + jax.random.randint(jax.random.fold_in(key, 33), (), 0, NSEGS - 1), NSEGS)
    short_by = short_by.at[first_pick].set(0)
    short_by = short_by.at[second_pick].set(SEG // 2 - 1)
    return (SEG - short_by).astype(jnp.int32)


def block_levels(stream_key, dims, shards, least, high):
    def one(axis_at, shards_of):
        heights = jax.random.uniform(jax.random.fold_in(jax.random.fold_in(stream_key, 6), axis_at), (shards_of,), jnp.float32, least / len(shards), high / len(shards))
        return jnp.repeat(jnp.exp(heights), dims[axis_at] // shards_of).reshape((-1,) + (1,) * (len(dims) - axis_at - 1))

    loudness = one(*shards[0])
    for cut in shards[1:]:
        loudness = loudness * one(*cut)
    return loudness


def centred(rng, shape, width, most, cuts=(), kind=jnp.bfloat16):
    result = width * jax.random.normal(rng, shape, jnp.float32)
    if cuts:
        result = result * block_levels(rng, shape, cuts, -0.22, 0.18)
    return jnp.clip(result, -most, most).astype(kind)


def setup_inputs(seed: int = 0) -> dict:
    key_of = jax.random.split(jax.random.key(seed), 8)
    return {
        "layer_input": draw_layer_input(jax.random.fold_in(key_of[7], 71), 0),
        "memory": centred(key_of[1], (N_SEQ, SEG, D), 1.0, 6.0, ((0, 8),)),
        "seg_lengths": draw_seg_lengths(jax.random.fold_in(key_of[7], 71), 0),
        "query_weight": draw_query_weight(jax.random.fold_in(key_of[7], 71), 0),
        "key_weight": draw_key_weight(jax.random.fold_in(key_of[7], 71), 0),
        "value_weight": centred(key_of[5], (D, D), D ** -0.5, 0.09375, ((1, 4),)),
        "out_weight": centred(key_of[6], (D, D), (D // 4) ** -0.5, 0.1875, ((0, 4),)),
    }


def attend_heads(queries, all_keys, all_values, key_ok):
    scores = jnp.einsum('qhd,khd->hqk', queries.astype(jnp.float32), all_keys.astype(jnp.float32)) / math.sqrt(HEAD_DIM)
    row_max = lax.optimization_barrier(jnp.max(jnp.where(key_ok[None], scores, -1e+30), axis=-1, keepdims=True))
    weights = jnp.where(key_ok[None], jnp.exp(scores - row_max), 0.0)
    probabilities = (weights / lax.optimization_barrier(jnp.sum(weights, axis=-1, keepdims=True))).astype(jnp.bfloat16)
    context = jnp.einsum('hqk,khd->qhd', probabilities.astype(jnp.float32), all_values.astype(jnp.float32))
    return context.astype(jnp.bfloat16)

def project(states, weight):
    return jnp.dot(states, weight, preferred_element_type=jnp.float32).astype(jnp.bfloat16)

def segment_step(inputs, mem_states, mem_len, own_len, query_weight, key_weight, value_weight, out_weight):
    seg_rows = inputs.shape[0]
    queries = project(inputs, query_weight).reshape(seg_rows, HEADS, HEAD_DIM)
    own_keys = project(inputs, key_weight).reshape(seg_rows, HEADS, HEAD_DIM)
    own_values = project(inputs, value_weight).reshape(seg_rows, HEADS, HEAD_DIM)
    mem_keys = project(mem_states, key_weight).reshape(seg_rows, HEADS, HEAD_DIM)
    mem_values = project(mem_states, value_weight).reshape(seg_rows, HEADS, HEAD_DIM)
    row_ids = jnp.arange(seg_rows, dtype=jnp.int32)[:, None]
    col_ids = jnp.arange(seg_rows, dtype=jnp.int32)[None, :]
    mem_ok = jnp.broadcast_to(col_ids < mem_len, (seg_rows, seg_rows))
    own_ok = (col_ids <= row_ids) & (col_ids < own_len)
    key_ok = jnp.concatenate([mem_ok, own_ok], axis=1)
    all_keys = jnp.concatenate([mem_keys, own_keys], axis=0)
    all_values = jnp.concatenate([mem_values, own_values], axis=0)
    context = attend_heads(queries, all_keys, all_values, key_ok).reshape(seg_rows, D)
    return jnp.dot(context, out_weight, preferred_element_type=jnp.float32).astype(jnp.bfloat16)

def reference(layer_input, memory, seg_lengths, query_weight, key_weight, value_weight, out_weight):

    def run_group(group_index):
        incoming = lax.dynamic_index_in_dim(memory, jnp.mod(group_index - 1, N_SEQ).astype(jnp.int32), 0, keepdims=False)
        mem_len = lax.dynamic_index_in_dim(seg_lengths, jnp.mod(group_index * SEGS_DEV - 1, NSEGS).astype(jnp.int32), 0, keepdims=False)
        results = []
        for seg_index in range(SEGS_DEV):
            position = (group_index * SEGS_DEV + seg_index).astype(jnp.int32)
            inputs = lax.dynamic_index_in_dim(layer_input, position, 0, keepdims=False)
            own_len = lax.dynamic_index_in_dim(seg_lengths, position, 0, keepdims=False)
            output = segment_step(inputs, incoming, mem_len, own_len, query_weight, key_weight, value_weight, out_weight)
            results.append(output)
            incoming = output
            mem_len = own_len
        return jnp.stack(results)
    grouped_out = lax.map(run_group, jnp.arange(N_SEQ, dtype=jnp.int32))
    return grouped_out.reshape(NSEGS, SEG, D)
```

```python
import functools
import math

import jax
import jax.numpy as jnp
from jax import lax
from jax.experimental import pallas as pl
from jax.experimental.pallas import tpu as pltpu
from jax.sharding import PartitionSpec as P

HEAD_DIM = 128
TILE = 256
PARTS = 4
VMEM = pltpu.VMEM
BF16 = jnp.bfloat16
F32 = jnp.float32


def dot(a, b):
    return jnp.dot(a, b, preferred_element_type=F32)


def tile_of(index, size):
    return pl.ds(pl.multiple_of(index * size, size), size)


def params(limit_mib):
    return pltpu.CompilerParams(vmem_limit_bytes=limit_mib << 20)


def cost(rows, depth, cols, extra=0):
    return pl.CostEstimate(
        flops=2 * rows * depth * cols,
        bytes_accessed=2 * (rows * depth + depth * cols + rows * cols) + extra,
        transcendentals=0,
    )


def streamed_kernel(x_hbm, w_hbm, out, x, w, x_sem, w_sem, tile_sem):
    depth, cols = w_hbm.shape
    part = depth // PARTS
    tiles = cols // TILE
    first = []
    for k in range(PARTS):
        rows = pl.ds(k * part, part)
        cx = pltpu.make_async_copy(x_hbm.at[:, rows], x.at[:, rows], x_sem.at[k])
        cw = pltpu.make_async_copy(
            w_hbm.at[rows, pl.ds(0, TILE)], w.at[0, rows, :], w_sem.at[k]
        )
        cx.start()
        cw.start()
        first.append((cx, cw))

    def fetch(j):
        return pltpu.make_async_copy(
            w_hbm.at[:, tile_of(j, TILE)], w.at[lax.rem(j, 2)], tile_sem.at[lax.rem(j, 2)]
        )

    if tiles > 1:
        fetch(1).start()
    total = None
    for k in range(PARTS):
        first[k][0].wait()
        first[k][1].wait()
        rows = pl.ds(k * part, part)
        term = dot(x[:, rows], w[0, rows, :])
        total = term if total is None else total + term
    out[:, pl.ds(0, TILE)] = total.astype(BF16)
    if tiles > 2:
        fetch(2).start()

    def step(j, carry):
        fetch(j).wait()
        out[:, tile_of(j, TILE)] = dot(x[...], w[lax.rem(j, 2)]).astype(BF16)

        @pl.when(j + 2 < tiles)
        def _():
            fetch(j + 2).start()

        return carry

    lax.fori_loop(1, tiles, step, 0)


def streamed(x, w):
    rows, depth = x.shape
    cols = w.shape[1]
    return pl.pallas_call(
        streamed_kernel,
        out_shape=jax.ShapeDtypeStruct((rows, cols), BF16),
        in_specs=[pl.BlockSpec(memory_space=pltpu.HBM)] * 2,
        out_specs=pl.BlockSpec(memory_space=VMEM),
        scratch_shapes=[
            VMEM((rows, depth), BF16),
            VMEM((2, depth, TILE), BF16),
            pltpu.SemaphoreType.DMA((PARTS,)),
            pltpu.SemaphoreType.DMA((PARTS,)),
            pltpu.SemaphoreType.DMA((2,)),
        ],
        compiler_params=params(12),
        cost_estimate=cost(rows, depth, cols),
    )(pltpu.with_memory_space_constraint(x, pltpu.HBM), pltpu.with_memory_space_constraint(w, pltpu.HBM))


def resident_kernel(count, x, *refs):
    cols = refs[0].shape[1]
    for w, out in zip(refs[:count], refs[count:]):

        def step(j, carry, w=w, out=out):
            out[:, tile_of(j, TILE)] = dot(x[...], w[:, tile_of(j, TILE)]).astype(BF16)
            return carry

        lax.fori_loop(0, cols // TILE, step, 0)


def resident(x, *ws):
    rows, depth = x.shape
    cols = ws[0].shape[1]
    count = len(ws)
    out = pl.pallas_call(
        functools.partial(resident_kernel, count),
        out_shape=[jax.ShapeDtypeStruct((rows, cols), BF16)] * count,
        in_specs=[pl.BlockSpec(memory_space=VMEM)] * (1 + count),
        out_specs=[pl.BlockSpec(memory_space=VMEM)] * count,
        compiler_params=params(4),
        cost_estimate=cost(rows, depth, cols * count),
    )(x, *ws)
    return out


def attend_kernel(blocks_of, split, lens, x, wq, km, vm, ko, vo, wo, *refs):
    blocks = blocks_of()
    outs = refs[: len(split)]
    q, bias, ctx = refs[len(split) :]
    rows = q.shape[0] // len(blocks)
    keys = ko.shape[0]
    width = wq.shape[1]
    group = lax.axis_index("seq")
    total = lens.shape[0]
    own_len = lens[group]
    mem_len = lens[lax.rem(group + total - 1, total)]
    tile = min(TILE, width)
    for n, b in enumerate(blocks):
        here = pl.ds(n * rows, rows)
        start = pl.multiple_of(b * rows, rows)
        row = lax.broadcasted_iota(jnp.int32, (rows, keys), 0) + start
        col = lax.broadcasted_iota(jnp.int32, (rows, keys), 1)
        bias[here, pl.ds(0, keys)] = jnp.where(col < mem_len, 0.0, -1e30)
        bias[here, pl.ds(keys, keys)] = jnp.where((col <= row) & (col < own_len), 0.0, -1e30)

    def project(j, carry):
        for n, b in enumerate(blocks):
            q[pl.ds(n * rows, rows), tile_of(j, tile)] = dot(
                x[tile_of(b, rows), :], wq[:, tile_of(j, tile)]
            ).astype(BF16)
        return carry

    lax.fori_loop(0, width // tile, project, 0)
    scale = math.log2(math.e) / math.sqrt(HEAD_DIM)

    def head(h, carry):
        lanes = tile_of(h, HEAD_DIM)
        query = q[:, lanes]
        nt = (((1,), (1,)), ((), ()))
        sm = lax.dot_general(query, km[:, lanes], nt, preferred_element_type=F32)
        so = lax.dot_general(query, ko[:, lanes], nt, preferred_element_type=F32)
        sm = sm + bias[:, pl.ds(0, keys)]
        so = so + bias[:, pl.ds(keys, keys)]
        top = jnp.maximum(
            jnp.max(sm, axis=-1, keepdims=True), jnp.max(so, axis=-1, keepdims=True)
        )
        pm = jnp.exp2((sm - top) * scale)
        po = jnp.exp2((so - top) * scale)
        norm = jnp.sum(pm, axis=-1, keepdims=True) + jnp.sum(po, axis=-1, keepdims=True)
        mixed = dot(pm.astype(BF16), vm[:, lanes]) + dot(po.astype(BF16), vo[:, lanes])
        ctx[:, lanes] = (mixed / norm).astype(BF16)
        return carry

    lax.fori_loop(0, width // HEAD_DIM, head, 0)
    for out, (block, first, cols) in zip(outs, split):
        here = pl.ds(block * rows, rows)

        def step(j, carry, out=out, here=here, first=first):
            out[:, tile_of(j, TILE)] = dot(
                ctx[here, :], wo[:, tile_of(j + first // TILE, TILE)]
            ).astype(out.dtype)
            return carry

        lax.fori_loop(0, cols // TILE, step, 0)


def attend(blocks_of, count, split, kinds, rows, lens, x, wq, km, vm, ko, vo, wo):
    keys = ko.shape[0]
    depth, width = wq.shape
    flops = 2 * count * rows * (2 * depth * width + 2 * width * 2 * keys)
    return pl.pallas_call(
        functools.partial(attend_kernel, blocks_of, split),
        out_shape=[
            jax.ShapeDtypeStruct((rows, cols), kind) for (_, _, cols), kind in zip(split, kinds)
        ],
        in_specs=[pl.BlockSpec(memory_space=pltpu.SMEM)] + [pl.BlockSpec(memory_space=VMEM)] * 7,
        out_specs=[pl.BlockSpec(memory_space=VMEM)] * len(split),
        scratch_shapes=[
            VMEM((count * rows, width), BF16),
            VMEM((count * rows, 2 * keys), F32),
            VMEM((count * rows, width), BF16),
        ],
        compiler_params=params(12),
        cost_estimate=pl.CostEstimate(
            flops=flops, bytes_accessed=4 * depth * width, transcendentals=0
        ),
    )(lens, x, wq, km, vm, ko, vo, wo)


def shifted(x, axis, by):
    devices = lax.axis_size(axis)
    return lax.ppermute(x, axis, [(i, (i + by) % devices) for i in range(devices)])


def swapped(x, bit):
    return lax.ppermute(x, "tp", [(i, i ^ bit) for i in range(lax.axis_size("tp"))])


def add_kernel(a, b, out):
    out[...] = (a[...] + b[...].astype(F32)).astype(BF16)


def add(a, b):
    return pl.pallas_call(
        add_kernel,
        out_shape=jax.ShapeDtypeStruct(a.shape, BF16),
        in_specs=[pl.BlockSpec(memory_space=VMEM)] * 2,
        out_specs=pl.BlockSpec(memory_space=VMEM),
        compiler_params=params(4),
        cost_estimate=pl.CostEstimate(flops=a.size, bytes_accessed=8 * a.size, transcendentals=0),
    )(a, b)


def final_kernel(own, xa, xb, ya, yb, out):
    half = xa.shape[1]
    left, right = pl.ds(0, half), pl.ds(half, half)
    out[0, :, left] = (own[:, left] + xa[...].astype(F32) + ya[...].astype(F32)).astype(BF16)
    out[0, :, right] = (own[:, right] + xb[...].astype(F32) + yb[...].astype(F32)).astype(BF16)


def final(own, *parts):
    return pl.pallas_call(
        final_kernel,
        out_shape=jax.ShapeDtypeStruct((1, *own.shape), BF16),
        in_specs=[pl.BlockSpec(memory_space=VMEM)] * 5,
        out_specs=pl.BlockSpec(memory_space=VMEM),
        compiler_params=params(4),
        cost_estimate=pl.CostEstimate(
            flops=3 * own.size, bytes_accessed=14 * own.size, transcendentals=0
        ),
    )(own, *parts)


def body(layer_input, memory, lens, wq, wk, wv, wo):
    seg_rows = layer_input.shape[1]
    shares = lax.axis_size("tp")
    x, m = layer_input[0], memory[0]
    rows = seg_rows // shares
    half = wo.shape[1] // 2
    sent_keys = streamed(m, wk)
    mem_keys = shifted(sent_keys, "seq", 1)
    (sent_values,) = resident(m, wv)
    mem_values = shifted(sent_values, "seq", 1)
    own_keys, own_values = resident(x, wk, wv)
    operands = (lens, x, wq, mem_keys, mem_values, own_keys, own_values, wo)

    if shares != 4:

        def every():
            return [jnp.int32(b) for b in range(shares)]

        terms = attend(
            every,
            shares,
            tuple((b, 0, 2 * half) for b in range(shares)),
            (F32,) * shares,
            rows,
            *operands,
        )
        summed = lax.psum_scatter(
            jnp.concatenate(terms), "tp", scatter_dimension=0, tiled=True
        )
        return summed.astype(BF16)[None]

    def far():
        return [lax.axis_index("tp") ^ 3]

    def near():
        return [lax.axis_index("tp") ^ 1, lax.axis_index("tp") ^ 2]

    def mine():
        return [lax.axis_index("tp")]

    far_a, far_b = attend(far, 1, ((0, 0, half), (0, half, half)), (BF16, BF16), rows, *operands)
    got_a, got_b = swapped(far_a, 1), swapped(far_b, 2)
    xa, xb, ya, yb = attend(
        near,
        2,
        ((0, 0, half), (0, half, half), (1, 0, half), (1, half, half)),
        (BF16, F32, F32, BF16),
        rows,
        *operands,
    )
    from_xa, from_yb = swapped(xa, 1), swapped(yb, 2)
    from_xb, from_ya = swapped(add(xb, got_b), 1), swapped(add(ya, got_a), 2)
    (own,) = attend(mine, 1, ((0, 0, 2 * half),), (F32,), rows, *operands)
    return final(own, from_xa, from_xb, from_ya, from_yb)


def solution(mesh):
    return jax.shard_map(
        body,
        mesh=mesh,
        in_specs=(
            P("seq", None, None),
            P("seq", None, None),
            P(),
            P(None, "tp"),
            P(None, "tp"),
            P(None, "tp"),
            P("tp", None),
        ),
        out_specs=P("seq", "tp", None),
        check_vma=False,
    )
```

```python
import functools
import math

import jax
import jax.numpy as jnp
from jax import lax
from jax.experimental import pallas as pl
from jax.experimental.pallas import tpu as pltpu
from jax.sharding import PartitionSpec as P


HEAD_DIM = 128
TILE = 256
PARTS = 8
VMEM = pltpu.VMEM
BF16 = jnp.bfloat16
F32 = jnp.float32


def dot(a, b):
    return jnp.dot(a, b, preferred_element_type=F32)


def tile_of(index, size):
    return pl.ds(pl.multiple_of(index * size, size), size)


def params(limit_mib):
    return pltpu.CompilerParams(vmem_limit_bytes=limit_mib << 20)


def cost(rows, depth, cols, extra=0):
    return pl.CostEstimate(
        flops=2 * rows * depth * cols,
        bytes_accessed=2 * (rows * depth + depth * cols + rows * cols) + extra,
        transcendentals=0,
    )


def streamed_kernel(x_hbm, w_hbm, out, x, w, total, x_sem, w_sem):
    depth, cols = w_hbm.shape
    part = depth // PARTS
    copies = []
    for k in range(PARTS):
        here = pl.ds(k * part, part)
        cx = pltpu.make_async_copy(x_hbm.at[:, here], x.at[:, here], x_sem.at[k])
        cw = pltpu.make_async_copy(w_hbm.at[here, :], w.at[here, :], w_sem.at[k])
        cx.start()
        cw.start()
        copies.append((cx, cw))
    for k in range(PARTS):
        copies[k][0].wait()
        copies[k][1].wait()
        here = pl.ds(k * part, part)
        for j in range(cols // TILE):
            lanes = pl.ds(j * TILE, TILE)
            term = dot(x[:, here], w[here, lanes])
            if k > 0:
                term = total[:, lanes] + term
            if k < PARTS - 1:
                total[:, lanes] = term
            else:
                out[:, lanes] = term.astype(BF16)


def streamed(x, w):
    rows, depth = x.shape
    cols = w.shape[1]
    return pl.pallas_call(
        streamed_kernel,
        out_shape=[jax.ShapeDtypeStruct(s, BF16) for s in ((rows, cols), x.shape, w.shape)],
        in_specs=[pl.BlockSpec(memory_space=pltpu.HBM)] * 2,
        out_specs=[pl.BlockSpec(memory_space=VMEM)] * 3,
        scratch_shapes=[
            VMEM((rows, cols), F32),
            pltpu.SemaphoreType.DMA((PARTS,)),
            pltpu.SemaphoreType.DMA((PARTS,)),
        ],
        compiler_params=params(4),
        cost_estimate=cost(rows, depth, cols),
    )(*(pltpu.with_memory_space_constraint(a, pltpu.HBM) for a in (x, w)))


def resident_kernel(count, x, *refs):
    cols = refs[0].shape[1]
    for w, out in zip(refs[:count], refs[count:]):

        def step(j, carry, w=w, out=out):
            out[:, tile_of(j, TILE)] = dot(x[...], w[:, tile_of(j, TILE)]).astype(BF16)
            return carry

        lax.fori_loop(0, cols // TILE, step, 0)


def resident(x, *ws):
    rows, depth = x.shape
    cols = ws[0].shape[1]
    count = len(ws)
    out = pl.pallas_call(
        functools.partial(resident_kernel, count),
        out_shape=[jax.ShapeDtypeStruct((rows, cols), BF16)] * count,
        in_specs=[pl.BlockSpec(memory_space=VMEM)] * (1 + count),
        out_specs=[pl.BlockSpec(memory_space=VMEM)] * count,
        compiler_params=params(4),
        cost_estimate=cost(rows, depth, cols * count),
    )(x, *ws)
    return out


def block_rows(b, rows):
    return pl.ds(b * rows, rows) if isinstance(b, int) else tile_of(b, rows)


def weigh_kernel(blocks_of, lens, q, km, ko, p, bias):
    blocks = blocks_of()
    width = q.shape[1]
    keys = ko.shape[0]
    rows = p.shape[1] // len(blocks)
    group = lax.axis_index("seq")
    total = lens.shape[0]
    own_len = lens[group]
    mem_len = lens[lax.rem(group + total - 1, total)]
    scale = math.log2(math.e) / math.sqrt(HEAD_DIM)
    nt = (((1,), (1,)), ((), ()))
    mem_cols, own_cols = pl.ds(0, keys), pl.ds(keys, keys)
    col = lax.broadcasted_iota(jnp.int32, (rows, keys), 1)
    bias[:, mem_cols] = jnp.where(col < mem_len, 0.0, -1e30)
    for n, b in enumerate(blocks):
        here = pl.ds(n * rows, rows)
        row = lax.broadcasted_iota(jnp.int32, (rows, keys), 0) + b * rows
        bias[:, own_cols] = jnp.where((col <= row) & (col < own_len), 0.0, -1e30)
        for h in range(width // HEAD_DIM):
            lanes = pl.ds(h * HEAD_DIM, HEAD_DIM)
            one = q[block_rows(b, rows), lanes]
            sm = lax.dot_general(one, km[:, lanes], nt, preferred_element_type=F32)
            so = lax.dot_general(one, ko[:, lanes], nt, preferred_element_type=F32)
            sm = sm + bias[:, mem_cols]
            so = so + bias[:, own_cols]
            top = jnp.maximum(
                jnp.max(sm, axis=-1, keepdims=True), jnp.max(so, axis=-1, keepdims=True)
            )
            pm = jnp.exp2((sm - top) * scale)
            po = jnp.exp2((so - top) * scale)
            norm = jnp.sum(pm, axis=-1, keepdims=True) + jnp.sum(po, axis=-1, keepdims=True)
            inverse = 1.0 / norm
            p[h, here, mem_cols] = (pm * inverse).astype(BF16)
            p[h, here, own_cols] = (po * inverse).astype(BF16)


def weigh(blocks_of, count, rows, lens, q, km, ko):
    width = q.shape[1]
    keys = ko.shape[0]
    heads = width // HEAD_DIM
    return pl.pallas_call(
        functools.partial(weigh_kernel, blocks_of),
        out_shape=jax.ShapeDtypeStruct((heads, count * rows, 2 * keys), BF16),
        in_specs=[pl.BlockSpec(memory_space=pltpu.SMEM)] + [pl.BlockSpec(memory_space=VMEM)] * 3,
        out_specs=pl.BlockSpec(memory_space=VMEM),
        scratch_shapes=[VMEM((rows, 2 * keys), F32)],
        compiler_params=params(8),
        cost_estimate=pl.CostEstimate(
            flops=4 * count * rows * width * keys,
            bytes_accessed=0,
            transcendentals=heads * count * rows * 2 * keys,
        ),
    )(lens, q, km, ko)


def attend_kernel(first, count, split, p, vm, vo, wo, *refs):
    outs = refs[: len(split)]
    (ctx,) = refs[len(split) :]
    rows = ctx.shape[0] // count
    keys, width = vo.shape
    here = pl.ds(first * rows, count * rows)
    for h in range(width // HEAD_DIM):
        lanes = pl.ds(h * HEAD_DIM, HEAD_DIM)
        mixed = dot(p[h, here, pl.ds(0, keys)], vm[:, lanes])
        mixed = mixed + dot(p[h, here, pl.ds(keys, keys)], vo[:, lanes])
        ctx[:, lanes] = mixed.astype(BF16)
    wide = 2 * TILE
    for j in range(wo.shape[1] // wide):
        term = dot(ctx[...], wo[:, pl.ds(j * wide, wide)])
        for out, (block, start, size) in zip(outs, split):
            if start <= j * wide < start + size:
                part = term[block * rows : (block + 1) * rows]
                out[:, pl.ds(j * wide - start, wide)] = part.astype(out.dtype)


def attend(first, count, split, kinds, rows, p, vm, vo, wo):
    keys, width = vo.shape
    depth = wo.shape[1]
    return pl.pallas_call(
        functools.partial(attend_kernel, first, count, split),
        out_shape=[
            jax.ShapeDtypeStruct((rows, cols), kind) for (_, _, cols), kind in zip(split, kinds)
        ],
        in_specs=[pl.BlockSpec(memory_space=VMEM)] * 4,
        out_specs=[pl.BlockSpec(memory_space=VMEM)] * len(split),
        scratch_shapes=[VMEM((count * rows, width), BF16)],
        compiler_params=params(8),
        cost_estimate=pl.CostEstimate(
            flops=2 * count * rows * width * (depth + 2 * keys),
            bytes_accessed=2 * depth * width,
            transcendentals=0,
        ),
    )(p, vm, vo, wo)


def shifted(x):
    devices = lax.axis_size("seq")
    return lax.ppermute(x, "seq", [(i, (i + 1) % devices) for i in range(devices)])


def swapped(x, bit):
    return lax.ppermute(x, "tp", [(i, i ^ bit) for i in range(lax.axis_size("tp"))])


def add_kernel(a, b, out):
    out[...] = (a[...] + b[...].astype(F32)).astype(BF16)


def add(a, b):
    return pl.pallas_call(
        add_kernel,
        out_shape=jax.ShapeDtypeStruct(a.shape, BF16),
        in_specs=[pl.BlockSpec(memory_space=VMEM)] * 2,
        out_specs=pl.BlockSpec(memory_space=VMEM),
        compiler_params=params(4),
        cost_estimate=pl.CostEstimate(flops=a.size, bytes_accessed=8 * a.size, transcendentals=0),
    )(a, b)


def final_kernel(own, xa, xb, ya, yb, out):
    half = xa.shape[1]
    left, right = pl.ds(0, half), pl.ds(half, half)
    out[0, :, left] = (own[:, left] + xa[...].astype(F32) + ya[...].astype(F32)).astype(BF16)
    out[0, :, right] = (own[:, right] + xb[...].astype(F32) + yb[...].astype(F32)).astype(BF16)


def final(own, *parts):
    return pl.pallas_call(
        final_kernel,
        out_shape=jax.ShapeDtypeStruct((1, *own.shape), BF16),
        in_specs=[pl.BlockSpec(memory_space=VMEM)] * 5,
        out_specs=pl.BlockSpec(memory_space=VMEM),
        compiler_params=params(4),
        cost_estimate=pl.CostEstimate(
            flops=3 * own.size, bytes_accessed=14 * own.size, transcendentals=0
        ),
    )(own, *parts)


def body(layer_input, memory, lens, wq, wk, wv, wo):
    seg_rows = layer_input.shape[1]
    shares = lax.axis_size("tp")
    x = layer_input[0]
    rows = seg_rows // shares
    half = wo.shape[1] // 2
    sent_keys, near_memory, near_wk = streamed(memory[0], wk)
    mem_keys = shifted(sent_keys)
    (sent_values,) = resident(near_memory, wv)
    mem_values = shifted(sent_values)
    own_keys, own_values, queries = resident(x, near_wk, wv, wq)
    sides = (lens, queries, mem_keys, own_keys)
    tail = (mem_values, own_values, wo)
    whole = (0, 2 * half)
    if shares != 4:
        p = weigh(lambda: list(range(shares)), shares, rows, *sides)
        split = tuple((b, *whole) for b in range(shares))
        terms = attend(0, shares, split, (F32,) * shares, rows, p, *tail)
        summed = lax.psum_scatter(
            jnp.concatenate(terms), "tp", scatter_dimension=0, tiled=True
        )
        return summed.astype(BF16)[None]

    def far():
        return [lax.axis_index("tp") ^ 3]

    def others():
        return [lax.axis_index("tp") ^ 1, lax.axis_index("tp") ^ 2, lax.axis_index("tp")]

    p_far = weigh(far, 1, rows, *sides)
    lower, upper = (0, half), (half, half)
    far_a, far_b = attend(0, 1, ((0, *lower), (0, *upper)), (BF16, BF16), rows, p_far, *tail)
    got_a, got_b = swapped(far_a, 1), swapped(far_b, 2)
    p_rest = weigh(others, 3, rows, *sides)
    split = ((0, *lower), (0, *upper), (1, *lower), (1, *upper))
    xa, xb, ya, yb = attend(0, 2, split, (BF16, F32, F32, BF16), rows, p_rest, *tail)
    from_xa, from_yb = swapped(xa, 1), swapped(yb, 2)
    from_xb, from_ya = swapped(add(xb, got_b), 1), swapped(add(ya, got_a), 2)
    (own,) = attend(2, 1, ((0, *whole),), (F32,), rows, p_rest, *tail)
    return final(own, from_xa, from_xb, from_ya, from_yb)


def solution(mesh):
    return jax.shard_map(
        body,
        mesh=mesh,
        in_specs=(
            P("seq", None, None),
            P("seq", None, None),
            P(),
            P(None, "tp"),
            P(None, "tp"),
            P(None, "tp"),
            P("tp", None),
        ),
        out_specs=P("seq", "tp", None),
        check_vma=False,
    )
```

```python
import functools
import math

import jax
import jax.numpy as jnp
from jax import lax
from jax.experimental import pallas as pl
from jax.experimental.pallas import tpu as pltpu
from jax.sharding import PartitionSpec as P


HEAD_DIM = 128
TILE = 256
PARTS = 8
VMEM = pltpu.VMEM
BF16 = jnp.bfloat16
F32 = jnp.float32


def dot(a, b):
    return jnp.dot(a, b, preferred_element_type=F32)


def tile_of(index, size):
    return pl.ds(pl.multiple_of(index * size, size), size)


def params(limit_mib):
    return pltpu.CompilerParams(vmem_limit_bytes=limit_mib << 20)


def cost(rows, depth, cols, extra=0):
    return pl.CostEstimate(
        flops=2 * rows * depth * cols,
        bytes_accessed=2 * (rows * depth + depth * cols + rows * cols) + extra,
        transcendentals=0,
    )


def streamed_kernel(start, x_hbm, w_hbm, out, w, *refs):
    depth, cols = w.shape
    part = depth // PARTS
    if len(refs) == 4:
        x, total, w_sem, x_sem = refs
    else:
        (total, w_sem), x, x_sem = refs, x_hbm, None
    copies = []
    for k in range(PARTS):
        here = pl.ds(k * part, part)
        source = w_hbm.at[here, pl.ds(start, cols)]
        both = [pltpu.make_async_copy(source, w.at[here, :], w_sem.at[k])]
        if x_sem is not None:
            both.append(pltpu.make_async_copy(x_hbm.at[:, here], x.at[:, here], x_sem.at[k]))
        for copy in both:
            copy.start()
        copies.append(both)
    for k in range(PARTS):
        for copy in copies[k]:
            copy.wait()
        here = pl.ds(k * part, part)
        for j in range(cols // TILE):
            lanes = pl.ds(j * TILE, TILE)
            term = dot(x[:, here], w[here, lanes])
            if k > 0:
                term = total[:, lanes] + term
            if k < PARTS - 1:
                total[:, lanes] = term
            else:
                out[:, lanes] = term.astype(BF16)


def streamed(x, w, start, cols, from_hbm):
    rows, depth = x.shape
    outs = ((rows, cols), (depth, cols)) + ((x.shape,) if from_hbm else ())
    space = pltpu.HBM if from_hbm else VMEM
    sems = [pltpu.SemaphoreType.DMA((PARTS,))] * (2 if from_hbm else 1)
    return pl.pallas_call(
        functools.partial(streamed_kernel, start),
        out_shape=[jax.ShapeDtypeStruct(s, BF16) for s in outs],
        in_specs=[pl.BlockSpec(memory_space=space), pl.BlockSpec(memory_space=pltpu.HBM)],
        out_specs=[pl.BlockSpec(memory_space=VMEM)] * len(outs),
        scratch_shapes=[VMEM((rows, cols), F32)] + sems,
        compiler_params=params(4),
        cost_estimate=cost(rows, depth, cols),
    )(
        pltpu.with_memory_space_constraint(x, pltpu.HBM) if from_hbm else x,
        pltpu.with_memory_space_constraint(w, pltpu.HBM),
    )


def resident_kernel(count, x, *refs):
    cols = refs[0].shape[1]
    for w, out in zip(refs[:count], refs[count:]):

        def step(j, carry, w=w, out=out):
            out[:, tile_of(j, TILE)] = dot(x[...], w[:, tile_of(j, TILE)]).astype(BF16)
            return carry

        lax.fori_loop(0, cols // TILE, step, 0)


def resident(x, *ws):
    rows, depth = x.shape
    cols = ws[0].shape[1]
    count = len(ws)
    out = pl.pallas_call(
        functools.partial(resident_kernel, count),
        out_shape=[jax.ShapeDtypeStruct((rows, cols), BF16)] * count,
        in_specs=[pl.BlockSpec(memory_space=VMEM)] * (1 + count),
        out_specs=[pl.BlockSpec(memory_space=VMEM)] * count,
        compiler_params=params(4),
        cost_estimate=cost(rows, depth, cols * count),
    )(x, *ws)
    return out


def block_rows(b, rows):
    return pl.ds(b * rows, rows) if isinstance(b, int) else tile_of(b, rows)


def own_kernel(blocks_of, x, wk_a, wk_b, wv, wq, k, v, q):
    blocks = blocks_of()
    rows = q.shape[0] // len(blocks)
    half = wk_a.shape[1]

    def key_step(j, carry):
        lanes = tile_of(j, TILE)
        k[:, lanes] = dot(x[...], wk_a[:, lanes]).astype(BF16)
        k[:, tile_of(j + half // TILE, TILE)] = dot(x[...], wk_b[:, lanes]).astype(BF16)
        return carry

    lax.fori_loop(0, half // TILE, key_step, 0)

    def step(j, carry):
        lanes = tile_of(j, TILE)
        v[:, lanes] = dot(x[...], wv[:, lanes]).astype(BF16)
        for n, b in enumerate(blocks):
            term = dot(x[block_rows(b, rows), :], wq[:, lanes])
            q[pl.ds(n * rows, rows), lanes] = term.astype(BF16)
        return carry

    lax.fori_loop(0, k.shape[1] // TILE, step, 0)


def own_projections(blocks_of, count, rows, x, wk_a, wk_b, wv, wq):
    total, depth = x.shape
    width = wv.shape[1]
    return pl.pallas_call(
        functools.partial(own_kernel, blocks_of),
        out_shape=[
            jax.ShapeDtypeStruct((r, width), BF16) for r in (total, total, count * rows)
        ],
        in_specs=[pl.BlockSpec(memory_space=VMEM)] * 5,
        out_specs=[pl.BlockSpec(memory_space=VMEM)] * 3,
        compiler_params=params(4),
        cost_estimate=cost(2 * total + count * rows, depth, width),
    )(x, wk_a, wk_b, wv, wq)


def queries_kernel(blocks_of, x, wq, q):
    blocks = blocks_of()
    rows = q.shape[0] // len(blocks)

    def step(j, carry):
        lanes = tile_of(j, TILE)
        for n, b in enumerate(blocks):
            term = dot(x[block_rows(b, rows), :], wq[:, lanes])
            q[pl.ds(n * rows, rows), lanes] = term.astype(BF16)
        return carry

    lax.fori_loop(0, q.shape[1] // TILE, step, 0)


def more_queries(blocks_of, count, rows, x, wq):
    depth, width = wq.shape
    return pl.pallas_call(
        functools.partial(queries_kernel, blocks_of),
        out_shape=jax.ShapeDtypeStruct((count * rows, width), BF16),
        in_specs=[pl.BlockSpec(memory_space=VMEM)] * 2,
        out_specs=pl.BlockSpec(memory_space=VMEM),
        compiler_params=params(4),
        cost_estimate=cost(count * rows, depth, width),
    )(x, wq)


def weigh_kernel(first, blocks_of, lens, q, km_a, km_b, ko, p, bias):
    blocks = blocks_of()
    width = q.shape[1]
    keys = ko.shape[0]
    rows = p.shape[1] // len(blocks)
    group = lax.axis_index("seq")
    total = lens.shape[0]
    own_len = lens[group]
    mem_len = lens[lax.rem(group + total - 1, total)]
    scale = math.log2(math.e) / math.sqrt(HEAD_DIM)
    nt = (((1,), (1,)), ((), ()))
    mem_cols, own_cols = pl.ds(0, keys), pl.ds(keys, keys)
    split = km_a.shape[1] // HEAD_DIM
    col = lax.broadcasted_iota(jnp.int32, (rows, keys), 1)
    bias[:, mem_cols] = jnp.where(col < mem_len, 0.0, -1e30)

    for n, b in enumerate(blocks):
        here = pl.ds(n * rows, rows)
        row = lax.broadcasted_iota(jnp.int32, (rows, keys), 0) + b * rows
        bias[:, own_cols] = jnp.where((col <= row) & (col < own_len), 0.0, -1e30)
        for h in range(width // HEAD_DIM):
            lanes = pl.ds(h * HEAD_DIM, HEAD_DIM)
            one = q[pl.ds((first + n) * rows, rows), lanes]
            km, at = (km_a, h) if h < split else (km_b, h - split)
            mem_lanes = pl.ds(at * HEAD_DIM, HEAD_DIM)
            sm = lax.dot_general(one, km[:, mem_lanes], nt, preferred_element_type=F32)
            so = lax.dot_general(one, ko[:, lanes], nt, preferred_element_type=F32)
            sm = sm + bias[:, mem_cols]
            so = so + bias[:, own_cols]
            top = jnp.maximum(
                jnp.max(sm, axis=-1, keepdims=True), jnp.max(so, axis=-1, keepdims=True)
            )
            pm = jnp.exp2((sm - top) * scale)
            po = jnp.exp2((so - top) * scale)
            norm = jnp.sum(pm, axis=-1, keepdims=True) + jnp.sum(po, axis=-1, keepdims=True)
            inverse = 1.0 / norm
            p[h, here, mem_cols] = (pm * inverse).astype(BF16)
            p[h, here, own_cols] = (po * inverse).astype(BF16)


def weigh(first, blocks_of, count, rows, lens, q, km_a, km_b, ko):
    width = q.shape[1]
    keys = ko.shape[0]
    heads = width // HEAD_DIM
    return pl.pallas_call(
        functools.partial(weigh_kernel, first, blocks_of),
        out_shape=jax.ShapeDtypeStruct((heads, count * rows, 2 * keys), BF16),
        in_specs=[pl.BlockSpec(memory_space=pltpu.SMEM)] + [pl.BlockSpec(memory_space=VMEM)] * 4,
        out_specs=pl.BlockSpec(memory_space=VMEM),
        scratch_shapes=[VMEM((rows, 2 * keys), F32)],
        compiler_params=params(4),
        cost_estimate=pl.CostEstimate(
            flops=4 * count * rows * width * keys,
            bytes_accessed=0,
            transcendentals=heads * count * rows * 2 * keys,
        ),
    )(lens, q, km_a, km_b, ko)


def context(p, vm, vo, ctx):
    keys, width = vo.shape
    for h in range(width // HEAD_DIM):
        lanes = pl.ds(h * HEAD_DIM, HEAD_DIM)
        mixed = dot(p[h, :, pl.ds(0, keys)], vm[:, lanes])
        mixed = mixed + dot(p[h, :, pl.ds(keys, keys)], vo[:, lanes])
        ctx[:, lanes] = mixed.astype(BF16)


def column_tiles(cols):
    wide = 2 * TILE
    return [(j, min(wide, cols - j)) for j in range(0, cols, wide)]


def attend_kernel(split, p, vm, vo, wo, *refs):
    outs, ctx = refs[:-1], refs[-1]
    context(p, vm, vo, ctx)
    rows = outs[0].shape[0]
    for out, (block, start, size) in zip(outs, split):
        for first, width in column_tiles(size):
            here = pl.ds(block * rows, rows)
            term = dot(ctx[here, :], wo[:, pl.ds(start + first, width)])
            out[:, pl.ds(first, width)] = term.astype(out.dtype)


def attend(count, split, kinds, rows, p, vm, vo, wo):
    keys, width = vo.shape
    depth = wo.shape[1]
    return pl.pallas_call(
        functools.partial(attend_kernel, split),
        out_shape=[
            jax.ShapeDtypeStruct((rows, cols), kind) for (_, _, cols), kind in zip(split, kinds)
        ],
        in_specs=[pl.BlockSpec(memory_space=VMEM)] * 4,
        out_specs=[pl.BlockSpec(memory_space=VMEM)] * len(split),
        scratch_shapes=[VMEM((count * rows, width), BF16)],
        compiler_params=params(4),
        cost_estimate=pl.CostEstimate(
            flops=2 * count * rows * width * (depth + 2 * keys),
            bytes_accessed=2 * depth * width,
            transcendentals=0,
        ),
    )(p, vm, vo, wo)


def direct_kernel(start, p, vm, vo, wo, out, ctx):
    context(p, vm, vo, ctx)
    for first, width in column_tiles(out.shape[1]):
        term = dot(ctx[...], wo[:, pl.ds(start + first, width)])
        out[:, pl.ds(first, width)] = term.astype(BF16)


def direct(start, cols, p, vm, vo, wo):
    keys, width = vo.shape
    rows = p.shape[1]
    return pl.pallas_call(
        functools.partial(direct_kernel, start),
        out_shape=[jax.ShapeDtypeStruct((rows, c), BF16) for c in (cols, width)],
        in_specs=[pl.BlockSpec(memory_space=VMEM)] * 4,
        out_specs=[pl.BlockSpec(memory_space=VMEM)] * 2,
        compiler_params=params(4),
        cost_estimate=pl.CostEstimate(
            flops=2 * rows * width * (cols + 2 * keys),
            bytes_accessed=2 * cols * width,
            transcendentals=0,
        ),
    )(p, vm, vo, wo)


def joined_kernel(start, ctx, wo, got, out):
    for first, width in column_tiles(out.shape[1]):
        here = pl.ds(first, width)
        term = dot(ctx[...], wo[:, pl.ds(start + first, width)])
        out[:, here] = (term + got[:, here].astype(F32)).astype(BF16)


def joined(start, ctx, wo, got):
    rows, width = ctx.shape
    return pl.pallas_call(
        functools.partial(joined_kernel, start),
        out_shape=jax.ShapeDtypeStruct(got.shape, BF16),
        in_specs=[pl.BlockSpec(memory_space=VMEM)] * 3,
        out_specs=pl.BlockSpec(memory_space=VMEM),
        compiler_params=params(4),
        cost_estimate=cost(rows, width, got.shape[1]),
    )(ctx, wo, got)


def to_next(x):
    devices = lax.axis_size("seq")
    return lax.ppermute(x, "seq", [(i, (i + 1) % devices) for i in range(devices)])


def swapped(x, bit):
    return lax.ppermute(x, "tp", [(i, i ^ bit) for i in range(lax.axis_size("tp"))])


def final_kernel(own, xa, xb, ya, yb, out_hbm, out, sems):
    rows, cut = xa.shape
    left, right = pl.ds(0, cut), pl.ds(cut, own.shape[1] - cut)
    part = rows // sems.shape[0]
    copies = []
    for k in range(sems.shape[0]):
        here = pl.ds(k * part, part)
        low = own[here, left] + xa[here, :].astype(F32) + ya[here, :].astype(F32)
        high = own[here, right] + xb[here, :].astype(F32) + yb[here, :].astype(F32)
        out[here, left] = low.astype(BF16)
        out[here, right] = high.astype(BF16)
        copy = pltpu.make_async_copy(out.at[here, :], out_hbm.at[0, here, :], sems.at[k])
        copy.start()
        copies.append(copy)
    for copy in copies:
        copy.wait()


def final(own, *parts):
    return pl.pallas_call(
        final_kernel,
        out_shape=jax.ShapeDtypeStruct((1, *own.shape), BF16),
        in_specs=[pl.BlockSpec(memory_space=VMEM)] * 5,
        out_specs=pl.BlockSpec(memory_space=pltpu.HBM),
        scratch_shapes=[VMEM(own.shape, BF16), pltpu.SemaphoreType.DMA((4,))],
        compiler_params=params(4),
        cost_estimate=pl.CostEstimate(
            flops=3 * own.size, bytes_accessed=14 * own.size, transcendentals=0
        ),
    )(own, *parts)


def body(layer_input, memory, lens, wq, wk, wv, wo):
    x = layer_input[0]
    shares = lax.axis_size("tp")
    rows = x.shape[0] // shares
    depth = wo.shape[1]
    cut = depth // 2 + HEAD_DIM
    whole, lower, upper = (0, depth), (0, cut), (cut, depth - cut)

    def block(bits):
        return lambda: [lax.axis_index("tp") ^ b for b in bits]

    part = wk.shape[1] // 2
    sent_a, wk_a, near_memory = streamed(memory[0], wk, 0, part, True)
    mem_keys_a = to_next(sent_a)
    sent_b, wk_b = streamed(near_memory, wk, part, part, False)
    mem_keys_b = to_next(sent_b)
    (sent_values,) = resident(near_memory, wv)
    mem_values = to_next(sent_values)
    weights = (wk_a, wk_b, wv, wq)
    if shares != 4:
        every = (lambda: list(range(shares)), shares, rows)
        own_keys, own_values, queries = own_projections(*every, x, *weights)
        p = weigh(0, *every, lens, queries, mem_keys_a, mem_keys_b, own_keys)
        split = tuple((b, *whole) for b in range(shares))
        terms = attend(shares, split, (F32,) * shares, rows, p, mem_values, own_values, wo)
        summed = lax.psum_scatter(
            jnp.concatenate(terms), "tp", scatter_dimension=0, tiled=True
        )
        return summed.astype(BF16)[None]

    own_keys, own_values, q_far = own_projections(block([3]), 1, rows, x, *weights)
    sides = (mem_keys_a, mem_keys_b, own_keys)
    tail = (mem_values, own_values, wo)
    p_far = weigh(0, block([3]), 1, rows, lens, q_far, *sides)
    far_a, far_b = attend(1, ((0, *lower), (0, *upper)), (BF16, BF16), rows, p_far, *tail)
    got_a = swapped(far_a, 1)
    got_b = swapped(far_b, 2)
    q_near = more_queries(block([1, 2]), 2, rows, x, wq)
    p_side = weigh(0, block([1]), 1, rows, lens, q_near, *sides)
    xa, side_ctx = direct(*lower, p_side, *tail)
    from_xa = swapped(xa, 1)
    q_near, side_ctx = lax.optimization_barrier((q_near, side_ctx))
    p_below = weigh(1, block([2]), 1, rows, lens, q_near, *sides)
    yb, below_ctx = direct(*upper, p_below, *tail)
    from_yb = swapped(yb, 2)
    xb = joined(cut, side_ctx, wo, got_b)
    ya = joined(0, below_ctx, wo, got_a)
    from_xb, from_ya = swapped(xb, 1), swapped(ya, 2)
    x, below_ctx = lax.optimization_barrier((x, below_ctx))
    q_mine = more_queries(block([0]), 1, rows, x, wq)
    p_mine = weigh(0, block([0]), 1, rows, lens, q_mine, *sides)
    (own,) = attend(1, ((0, *whole),), (F32,), rows, p_mine, *tail)
    return final(own, from_xa, from_xb, from_ya, from_yb)


def solution(mesh):
    return jax.shard_map(
        body,
        mesh=mesh,
        in_specs=(
            P("seq", None, None),
            P("seq", None, None),
            P(),
            P(None, "tp"),
            P(None, "tp"),
            P(None, "tp"),
            P("tp", None),
        ),
        out_specs=P("seq", "tp", None),
        check_vma=False,
    )
```

```python
import functools
import math

import jax
import jax.numpy as jnp
from jax import lax
from jax.experimental import pallas as pl
from jax.experimental.pallas import tpu as pltpu
from jax.sharding import PartitionSpec as P


HEAD_DIM = 128
TILE = 256
PARTS = 8
VMEM = pltpu.VMEM
BF16 = jnp.bfloat16
F32 = jnp.float32


def dot(a, b):
    return jnp.dot(a, b, preferred_element_type=F32)


def tile_of(index, size):
    return pl.ds(pl.multiple_of(index * size, size), size)


def params(limit_mib):
    return pltpu.CompilerParams(vmem_limit_bytes=limit_mib << 20)


def cost(rows, depth, cols, extra=0):
    return pl.CostEstimate(
        flops=2 * rows * depth * cols,
        bytes_accessed=2 * (rows * depth + depth * cols + rows * cols) + extra,
        transcendentals=0,
    )


def streamed_kernel(start, x_hbm, w_hbm, out, w, *refs):
    depth, cols = w.shape
    part = depth // PARTS
    if len(refs) == 4:
        x, total, w_sem, x_sem = refs
    else:
        (total, w_sem), x, x_sem = refs, x_hbm, None
    copies = []
    for k in range(PARTS):
        here = pl.ds(k * part, part)
        source = w_hbm.at[here, pl.ds(start, cols)]
        both = [pltpu.make_async_copy(source, w.at[here, :], w_sem.at[k])]
        if x_sem is not None:
            both.append(pltpu.make_async_copy(x_hbm.at[:, here], x.at[:, here], x_sem.at[k]))
        for copy in both:
            copy.start()
        copies.append(both)
    for k in range(PARTS):
        for copy in copies[k]:
            copy.wait()
        here = pl.ds(k * part, part)
        for j in range(cols // TILE):
            lanes = pl.ds(j * TILE, TILE)
            term = dot(x[:, here], w[here, lanes])
            if k > 0:
                term = total[:, lanes] + term
            if k < PARTS - 1:
                total[:, lanes] = term
            else:
                out[:, lanes] = term.astype(BF16)


def streamed(x, w, start, cols, from_hbm):
    rows, depth = x.shape
    outs = ((rows, cols), (depth, cols)) + ((x.shape,) if from_hbm else ())
    space = pltpu.HBM if from_hbm else VMEM
    sems = [pltpu.SemaphoreType.DMA((PARTS,))] * (2 if from_hbm else 1)
    return pl.pallas_call(
        functools.partial(streamed_kernel, start),
        out_shape=[jax.ShapeDtypeStruct(s, BF16) for s in outs],
        in_specs=[pl.BlockSpec(memory_space=space), pl.BlockSpec(memory_space=pltpu.HBM)],
        out_specs=[pl.BlockSpec(memory_space=VMEM)] * len(outs),
        scratch_shapes=[VMEM((rows, cols), F32)] + sems,
        compiler_params=params(4),
        cost_estimate=cost(rows, depth, cols),
    )(
        pltpu.with_memory_space_constraint(x, pltpu.HBM) if from_hbm else x,
        pltpu.with_memory_space_constraint(w, pltpu.HBM),
    )


def resident_kernel(count, x, *refs):
    cols = refs[0].shape[1]
    wide = min(2 * TILE, cols)
    for w, out in zip(refs[:count], refs[count:]):

        def step(j, carry, w=w, out=out):
            out[:, tile_of(j, wide)] = dot(x[...], w[:, tile_of(j, wide)]).astype(BF16)
            return carry

        lax.fori_loop(0, cols // wide, step, 0)


def resident(x, *ws):
    rows, depth = x.shape
    cols = ws[0].shape[1]
    count = len(ws)
    out = pl.pallas_call(
        functools.partial(resident_kernel, count),
        out_shape=[jax.ShapeDtypeStruct((rows, cols), BF16)] * count,
        in_specs=[pl.BlockSpec(memory_space=VMEM)] * (1 + count),
        out_specs=[pl.BlockSpec(memory_space=VMEM)] * count,
        compiler_params=params(4),
        cost_estimate=cost(rows, depth, cols * count),
    )(x, *ws)
    return out


def block_rows(b, rows):
    return pl.ds(b * rows, rows) if isinstance(b, int) else tile_of(b, rows)


def own_kernel(blocks_of, x, wk_a, wk_b, wv, wq, k, v, q):
    blocks = blocks_of()
    rows = q.shape[0] // len(blocks)
    half = wk_a.shape[1]
    k[:, pl.ds(0, half)] = dot(x[...], wk_a[...]).astype(BF16)
    k[:, pl.ds(half, half)] = dot(x[...], wk_b[...]).astype(BF16)
    wide = min(2 * TILE, wv.shape[1])

    def step(j, carry):
        lanes = tile_of(j, wide)
        v[:, lanes] = dot(x[...], wv[:, lanes]).astype(BF16)
        for n, b in enumerate(blocks):
            term = dot(x[block_rows(b, rows), :], wq[:, lanes])
            q[pl.ds(n * rows, rows), lanes] = term.astype(BF16)
        return carry

    lax.fori_loop(0, k.shape[1] // wide, step, 0)


def own_projections(blocks_of, count, rows, x, wk_a, wk_b, wv, wq):
    total, depth = x.shape
    width = wv.shape[1]
    return pl.pallas_call(
        functools.partial(own_kernel, blocks_of),
        out_shape=[
            jax.ShapeDtypeStruct((r, width), BF16) for r in (total, total, count * rows)
        ],
        in_specs=[pl.BlockSpec(memory_space=VMEM)] * 5,
        out_specs=[pl.BlockSpec(memory_space=VMEM)] * 3,
        compiler_params=params(4),
        cost_estimate=cost(2 * total + count * rows, depth, width),
    )(x, wk_a, wk_b, wv, wq)


def queries_kernel(blocks_of, x, wq, q):
    blocks = blocks_of()
    rows = q.shape[0] // len(blocks)
    wide = min(2 * TILE, q.shape[1])

    def step(j, carry):
        lanes = tile_of(j, wide)
        for n, b in enumerate(blocks):
            term = dot(x[block_rows(b, rows), :], wq[:, lanes])
            q[pl.ds(n * rows, rows), lanes] = term.astype(BF16)
        return carry

    lax.fori_loop(0, q.shape[1] // wide, step, 0)


def more_queries(blocks_of, count, rows, x, wq):
    depth, width = wq.shape
    return pl.pallas_call(
        functools.partial(queries_kernel, blocks_of),
        out_shape=jax.ShapeDtypeStruct((count * rows, width), BF16),
        in_specs=[pl.BlockSpec(memory_space=VMEM)] * 2,
        out_specs=pl.BlockSpec(memory_space=VMEM),
        compiler_params=params(4),
        cost_estimate=cost(count * rows, depth, width),
    )(x, wq)


def weigh_kernel(first, blocks_of, lens, q, km_a, km_b, ko, p, bias):
    blocks = blocks_of()
    width = q.shape[1]
    keys = ko.shape[0]
    rows = p.shape[1] // len(blocks)
    group = lax.axis_index("seq")
    total = lens.shape[0]
    own_len = lens[group]
    mem_len = lens[lax.rem(group + total - 1, total)]
    scale = math.log2(math.e) / math.sqrt(HEAD_DIM)
    nt = (((1,), (1,)), ((), ()))
    mem_cols, own_cols = pl.ds(0, keys), pl.ds(keys, keys)
    split = km_a.shape[1] // HEAD_DIM
    col = lax.broadcasted_iota(jnp.int32, (rows, keys), 1)
    bias[:, mem_cols] = jnp.where(col < mem_len, 0.0, -1e30)

    for n, b in enumerate(blocks):
        here = pl.ds(n * rows, rows)
        row = lax.broadcasted_iota(jnp.int32, (rows, keys), 0) + b * rows
        bias[:, own_cols] = jnp.where((col <= row) & (col < own_len), 0.0, -1e30)
        for h in range(width // HEAD_DIM):
            lanes = pl.ds(h * HEAD_DIM, HEAD_DIM)
            one = q[pl.ds((first + n) * rows, rows), lanes]
            km, at = (km_a, h) if h < split else (km_b, h - split)
            mem_lanes = pl.ds(at * HEAD_DIM, HEAD_DIM)
            sm = lax.dot_general(one, km[:, mem_lanes], nt, preferred_element_type=F32)
            so = lax.dot_general(one, ko[:, lanes], nt, preferred_element_type=F32)
            sm = sm + bias[:, mem_cols]
            so = so + bias[:, own_cols]
            top = jnp.maximum(
                jnp.max(sm, axis=-1, keepdims=True), jnp.max(so, axis=-1, keepdims=True)
            )
            pm = jnp.exp2((sm - top) * scale)
            po = jnp.exp2((so - top) * scale)
            norm = jnp.sum(pm, axis=-1, keepdims=True) + jnp.sum(po, axis=-1, keepdims=True)
            inverse = 1.0 / norm
            p[h, here, mem_cols] = (pm * inverse).astype(BF16)
            p[h, here, own_cols] = (po * inverse).astype(BF16)


def weigh(first, blocks_of, count, rows, lens, q, km_a, km_b, ko):
    width = q.shape[1]
    keys = ko.shape[0]
    heads = width // HEAD_DIM
    return pl.pallas_call(
        functools.partial(weigh_kernel, first, blocks_of),
        out_shape=jax.ShapeDtypeStruct((heads, count * rows, 2 * keys), BF16),
        in_specs=[pl.BlockSpec(memory_space=pltpu.SMEM)] + [pl.BlockSpec(memory_space=VMEM)] * 4,
        out_specs=pl.BlockSpec(memory_space=VMEM),
        scratch_shapes=[VMEM((rows, 2 * keys), F32)],
        compiler_params=params(4),
        cost_estimate=pl.CostEstimate(
            flops=4 * count * rows * width * keys,
            bytes_accessed=0,
            transcendentals=heads * count * rows * 2 * keys,
        ),
    )(lens, q, km_a, km_b, ko)


def context(p, vm, vo, ctx):
    keys, width = vo.shape
    for h in range(width // HEAD_DIM):
        lanes = pl.ds(h * HEAD_DIM, HEAD_DIM)
        mixed = dot(p[h, :, pl.ds(0, keys)], vm[:, lanes])
        mixed = mixed + dot(p[h, :, pl.ds(keys, keys)], vo[:, lanes])
        ctx[:, lanes] = mixed.astype(BF16)


def column_tiles(cols):
    wide = 2 * TILE
    return [(j, min(wide, cols - j)) for j in range(0, cols, wide)]


def attend_kernel(split, p, vm, vo, wo, *refs):
    outs, ctx = refs[:-1], refs[-1]
    context(p, vm, vo, ctx)
    rows = outs[0].shape[0]
    for out, (block, start, size) in zip(outs, split):
        for first, width in column_tiles(size):
            here = pl.ds(block * rows, rows)
            term = dot(ctx[here, :], wo[:, pl.ds(start + first, width)])
            out[:, pl.ds(first, width)] = term.astype(out.dtype)


def attend(count, split, kinds, rows, p, vm, vo, wo):
    keys, width = vo.shape
    depth = wo.shape[1]
    return pl.pallas_call(
        functools.partial(attend_kernel, split),
        out_shape=[
            jax.ShapeDtypeStruct((rows, cols), kind) for (_, _, cols), kind in zip(split, kinds)
        ],
        in_specs=[pl.BlockSpec(memory_space=VMEM)] * 4,
        out_specs=[pl.BlockSpec(memory_space=VMEM)] * len(split),
        scratch_shapes=[VMEM((count * rows, width), BF16)],
        compiler_params=params(4),
        cost_estimate=pl.CostEstimate(
            flops=2 * count * rows * width * (depth + 2 * keys),
            bytes_accessed=2 * depth * width,
            transcendentals=0,
        ),
    )(p, vm, vo, wo)


def direct_kernel(start, p, vm, vo, wo, out, ctx):
    context(p, vm, vo, ctx)
    for first, width in column_tiles(out.shape[1]):
        term = dot(ctx[...], wo[:, pl.ds(start + first, width)])
        out[:, pl.ds(first, width)] = term.astype(BF16)


def direct(start, cols, p, vm, vo, wo):
    keys, width = vo.shape
    rows = p.shape[1]
    return pl.pallas_call(
        functools.partial(direct_kernel, start),
        out_shape=[jax.ShapeDtypeStruct((rows, c), BF16) for c in (cols, width)],
        in_specs=[pl.BlockSpec(memory_space=VMEM)] * 4,
        out_specs=[pl.BlockSpec(memory_space=VMEM)] * 2,
        compiler_params=params(4),
        cost_estimate=pl.CostEstimate(
            flops=2 * rows * width * (cols + 2 * keys),
            bytes_accessed=2 * cols * width,
            transcendentals=0,
        ),
    )(p, vm, vo, wo)


def joined_kernel(start, ctx, wo, got, out):
    for first, width in column_tiles(out.shape[1]):
        here = pl.ds(first, width)
        term = dot(ctx[...], wo[:, pl.ds(start + first, width)])
        out[:, here] = (term + got[:, here].astype(F32)).astype(BF16)


def joined(start, ctx, wo, got):
    rows, width = ctx.shape
    return pl.pallas_call(
        functools.partial(joined_kernel, start),
        out_shape=jax.ShapeDtypeStruct(got.shape, BF16),
        in_specs=[pl.BlockSpec(memory_space=VMEM)] * 3,
        out_specs=pl.BlockSpec(memory_space=VMEM),
        compiler_params=params(4),
        cost_estimate=cost(rows, width, got.shape[1]),
    )(ctx, wo, got)


def to_next(x):
    devices = lax.axis_size("seq")
    return lax.ppermute(x, "seq", [(i, (i + 1) % devices) for i in range(devices)])


def swapped(x, bit):
    return lax.ppermute(x, "tp", [(i, i ^ bit) for i in range(lax.axis_size("tp"))])


def final_kernel(own, xa, xb, ya, yb, out_hbm, out, sems):
    rows, cut = xa.shape
    left, right = pl.ds(0, cut), pl.ds(cut, own.shape[1] - cut)
    part = rows // sems.shape[0]
    copies = []
    for k in range(sems.shape[0]):
        here = pl.ds(k * part, part)
        low = own[here, left] + xa[here, :].astype(F32) + ya[here, :].astype(F32)
        high = own[here, right] + xb[here, :].astype(F32) + yb[here, :].astype(F32)
        out[here, left] = low.astype(BF16)
        out[here, right] = high.astype(BF16)
        copy = pltpu.make_async_copy(out.at[here, :], out_hbm.at[0, here, :], sems.at[k])
        copy.start()
        copies.append(copy)
    for copy in copies:
        copy.wait()


def final(own, *parts):
    return pl.pallas_call(
        final_kernel,
        out_shape=jax.ShapeDtypeStruct((1, *own.shape), BF16),
        in_specs=[pl.BlockSpec(memory_space=VMEM)] * 5,
        out_specs=pl.BlockSpec(memory_space=pltpu.HBM),
        scratch_shapes=[VMEM(own.shape, BF16), pltpu.SemaphoreType.DMA((4,))],
        compiler_params=params(4),
        cost_estimate=pl.CostEstimate(
            flops=3 * own.size, bytes_accessed=14 * own.size, transcendentals=0
        ),
    )(own, *parts)


def body(layer_input, memory, lens, wq, wk, wv, wo):
    x = layer_input[0]
    shares = lax.axis_size("tp")
    rows = x.shape[0] // shares
    depth = wo.shape[1]
    cut = depth // 2 + 2 * HEAD_DIM
    whole, lower, upper = (0, depth), (0, cut), (cut, depth - cut)

    def block(bits):
        return lambda: [lax.axis_index("tp") ^ b for b in bits]

    part = wk.shape[1] // 2
    sent_a, wk_a, near_memory = streamed(memory[0], wk, 0, part, True)
    mem_keys_a = to_next(sent_a)
    sent_b, wk_b = streamed(near_memory, wk, part, part, False)
    mem_keys_b = to_next(sent_b)
    (sent_values,) = resident(near_memory, wv)
    mem_values = to_next(sent_values)
    weights = (wk_a, wk_b, wv, wq)
    if shares != 4:
        every = (lambda: list(range(shares)), shares, rows)
        own_keys, own_values, queries = own_projections(*every, x, *weights)
        p = weigh(0, *every, lens, queries, mem_keys_a, mem_keys_b, own_keys)
        split = tuple((b, *whole) for b in range(shares))
        terms = attend(shares, split, (F32,) * shares, rows, p, mem_values, own_values, wo)
        summed = lax.psum_scatter(
            jnp.concatenate(terms), "tp", scatter_dimension=0, tiled=True
        )
        return summed.astype(BF16)[None]

    own_keys, own_values, q_far = own_projections(block([3]), 1, rows, x, *weights)
    sides = (mem_keys_a, mem_keys_b, own_keys)
    tail = (mem_values, own_values, wo)
    p_far = weigh(0, block([3]), 1, rows, lens, q_far, *sides)
    far_a, far_b = attend(1, ((0, *lower), (0, *upper)), (BF16, BF16), rows, p_far, *tail)
    got_a = swapped(far_a, 1)
    got_b = swapped(far_b, 2)
    q_near = more_queries(block([1, 2]), 2, rows, x, wq)
    p_side = weigh(0, block([1]), 1, rows, lens, q_near, *sides)
    xa, side_ctx = direct(*lower, p_side, *tail)
    from_xa = swapped(xa, 1)
    q_near, side_ctx = lax.optimization_barrier((q_near, side_ctx))
    p_below = weigh(1, block([2]), 1, rows, lens, q_near, *sides)
    yb, below_ctx = direct(*upper, p_below, *tail)
    from_yb = swapped(yb, 2)
    xb = joined(cut, side_ctx, wo, got_b)
    ya = joined(0, below_ctx, wo, got_a)
    from_xb, from_ya = swapped(xb, 1), swapped(ya, 2)
    x, below_ctx = lax.optimization_barrier((x, below_ctx))
    q_mine = more_queries(block([0]), 1, rows, x, wq)
    p_mine = weigh(0, block([0]), 1, rows, lens, q_mine, *sides)
    (own,) = attend(1, ((0, *whole),), (F32,), rows, p_mine, *tail)
    return final(own, from_xa, from_xb, from_ya, from_yb)


def solution(mesh):
    return jax.shard_map(
        body,
        mesh=mesh,
        in_specs=(
            P("seq", None, None),
            P("seq", None, None),
            P(),
            P(None, "tp"),
            P(None, "tp"),
            P(None, "tp"),
            P("tp", None),
        ),
        out_specs=P("seq", "tp", None),
        check_vma=False,
    )
```
